256 devices in a mesh: site: 2 (over core), wide: 32 (over x, z), narrow: 4 (over y).
Axes of the slice: x: 4, y: 4, z: 8, core: 2. Of those that a mesh axis runs over, the one named last changes fastest.
Arguments:
- initial_rows: float32 [64, 4, 2048], P('site', 'narrow'), may hold values from -6 to 6
- outcomes: int32 [64, 4], replicated, may hold values 0 or 1
- tensors: float32 [4, 2, 4, 2048, 8192], P('site', None, 'narrow', None, 'wide'), may hold values from -0.25 to 0.25
Outputs:
- final_rows: float32 [64, 4, 2048], P('site', 'narrow')
- log_weight: float32 [64], P('site')
The draws below stay inside these ranges and needn't reach their ends.
All inputs are finite; a program needn't handle non-finite values.
Results may differ from the reference program's by a relative error of at most 0.0003.
Values sent between devices are 32-bit elements; how exact they have to be, the bound alone decides.
A program may use at most 64 MiB of HBM per device.

```python
import math
import jax
import jax.numpy as jnp
from jax import lax

BOND = 8192
SITES = 4
SAMPLES = 64
N_NARROW = 4


def draw_tensors(key, part):
    shape = (SITES, 2, N_NARROW, BOND // N_NARROW, BOND)
    base_key, column_key = jax.random.split(jax.random.fold_in(key, 11))
    base = jnp.clip(jax.random.normal(base_key, shape, jnp.float32), -6.0, 6.0)
    spread = jnp.exp(jax.random.uniform(column_key, (SITES, 2, 1, 1, BOND), jnp.float32, 0.0, math.log(10.0)))
    rising = jnp.exp(math.log(3.0) * jnp.arange(BOND, dtype=jnp.float32) / BOND)
    return jnp.clip(base * spread * rising / (3.0 * math.sqrt(BOND)), -0.25, 0.25)


def plant(entries, stream_key, low, high):
    dims = entries.shape
    place = [jax.random.randint(jax.random.fold_in(stream_key, axis), (), 0, dims[axis]) for axis in range(len(dims))]
    entries = entries.at[tuple(place)].set(low)
    longest = dims.index(max(dims))
    place[longest] = (place[longest] + 1) % dims[longest]
    return entries.at[tuple(place)].set(high)


def levels(stream_key, dims, pieces, low, largest):
    level = 1.0
    for dim, blocks in pieces:
        heights = jax.random.uniform(jax.random.fold_in(jax.random.fold_in(stream_key, 6), dim), (blocks,), jnp.float32, low / len(pieces), largest / len(pieces))
        level = level * jnp.repeat(jnp.exp(heights), dims[dim] // blocks).reshape((-1,) + (1,) * (len(dims) - 1 - dim))
    return level


def noise(key, extent, scale, limit, cuts=(), held_as=jnp.bfloat16):
    level = levels(key, extent, cuts, -0.22, 0.18) if cuts else 1.0
    drawn = jax.random.normal(key, extent, jnp.float32) * scale * level
    return jnp.minimum(jnp.maximum(drawn, -limit), limit).astype(held_as)


def setup_inputs(seed: int = 0) -> dict:
    seeds = jax.random.split(jax.random.key(seed), 4)
    initial_rows = noise(seeds[0], (SAMPLES, N_NARROW, BOND // N_NARROW), 1.0, 6.0, ((0, 2), (1, 4)), jnp.float32)
    outcomes = plant((jax.random.randint(seeds[1], (SAMPLES, SITES), 0, 2) < 1).astype(jnp.int32), jax.random.fold_in(seeds[1], 1), 0, 1)
    tensors = draw_tensors(jax.random.fold_in(seeds[3], 71), 0)
    return dict(initial_rows=initial_rows, outcomes=outcomes, tensors=tensors)


epsilon = 1e-06

def reference(initial_rows, outcomes, tensors):
    samples = initial_rows.shape[0]
    state = initial_rows.reshape(samples, BOND)
    log_weight = jnp.zeros((samples,), jnp.float32)
    for site_index in range(SITES):
        site_tensor = tensors[site_index].reshape(2, BOND, BOND)
        first = jnp.dot(state, site_tensor[0], precision=lax.Precision.HIGHEST, preferred_element_type=jnp.float32)
        second = jnp.dot(state, site_tensor[1], precision=lax.Precision.HIGHEST, preferred_element_type=jnp.float32)
        square_first = lax.optimization_barrier(jnp.sum(first * first, axis=1))
        square_second = lax.optimization_barrier(jnp.sum(second * second, axis=1))
        chosen = outcomes[:, site_index]
        both_mean = (square_first + square_second) / (2.0 * BOND)
        kept_square = jnp.where(chosen == 0, square_first, square_second)
        kept = jnp.where(chosen[:, None] == 0, first, second)
        state = kept * lax.rsqrt(both_mean + epsilon)[:, None]
        log_weight = log_weight + jnp.log(kept_square / BOND + epsilon) - jnp.log(both_mean + epsilon)
    return (state.reshape(samples, N_NARROW, BOND // N_NARROW), log_weight)
```

```python
import functools

import jax
import jax.numpy as jnp
from jax import lax
from jax.experimental import pallas as pl
from jax.experimental.pallas import tpu as pltpu
from jax.sharding import PartitionSpec as P

MESH = pl.DeviceIdType.MESH
EPSILON = 1e-06
STEPS = 4
BLOCK = 256
GROUP = 16
HALF = 8
LANES = 128


def split_value(value):
    high = value.astype(jnp.bfloat16)
    low = (value - high.astype(jnp.float32)).astype(jnp.bfloat16)
    return high, low


def near_first(extent):
    return sorted(range(1, extent), key=lambda d: min(d, extent - d))


def kernel(
    xn,
    zn,
    bond,
    x_hbm,
    oc_ref,
    t_hbm,
    raw_ref,
    aux_ref,
    t32,
    thi,
    tlo,
    xin,
    psend,
    rsb,
    st,
    stf,
    yex,
    yexf,
    ysend,
    t_sem,
    x_sem,
    f_sem,
    rs_send,
    rs_recv,
    z_send,
    z_recv,
    x_send,
    x_recv,
    y_send,
    y_recv,
):
    s = lax.axis_index("site")
    w = lax.axis_index("wide")
    y = lax.axis_index("narrow")
    x = lax.div(w, zn)
    z = lax.rem(w, zn)
    fronts = xn * HALF
    z_order = near_first(zn)

    def dev(site, xx, yy, zz):
        return (site, xx * zn + zz, yy)

    def around(value, offset, extent):
        return lax.rem(value + offset, extent)

    def remote(src, dst, send, recv, where):
        return pltpu.make_async_remote_copy(
            src_ref=src, dst_ref=dst, send_sem=send, recv_sem=recv, device_id=where, device_id_type=MESH
        )

    rows_k = zn * BLOCK
    t_chunk = min(rows_k, 512)
    chunks = rows_k // t_chunk

    def t_copy(site, c):
        rows = pl.ds(c * t_chunk, t_chunk)
        return pltpu.make_async_copy(t_hbm.at[site, :, 0, rows, :], t32.at[site, :, rows, :], t_sem.at[site, c])

    for c in range(chunks):
        t_copy(0, c).start()
    own_rows = pltpu.make_async_copy(x_hbm, xin.at[0], x_sem)

    @pl.when(s == 0)
    def _():
        own_rows.start()

    for c in range(chunks):
        t_copy(1, c).start()

    barrier = pltpu.get_barrier_semaphore()
    peers = 0
    for ds in range(2):
        for dx in range(xn):
            for dy in range(xn):
                if ds or dx or dy:
                    pl.semaphore_signal(
                        barrier,
                        inc=1,
                        device_id=dev(around(s, ds, 2), around(x, dx, xn), around(y, dy, xn), z),
                        device_id_type=MESH,
                    )
                    peers += 1
    for d in range(1, zn):
        pl.semaphore_signal(barrier, inc=1, device_id=dev(s, x, y, around(z, d, zn)), device_id_type=MESH)
        peers += 1
    pl.semaphore_wait(barrier, peers)

    def split_rows(site, start):
        for o in range(2):
            rows = pl.ds(start, BLOCK)
            high, low = split_value(t32[site, o, rows, :])
            thi[site, o, rows, :] = high
            tlo[site, o, rows, :] = low

    def block_product(lhs, site, start):
        high, low = split_value(lhs)
        both = jnp.concatenate([high, low], axis=0)
        n = lhs.shape[0]
        rows = pl.ds(start, BLOCK)
        out = []
        for o in range(2):
            t_high, t_low = thi[site, o, rows, :], tlo[site, o, rows, :]
            main = jnp.dot(both, t_high, preferred_element_type=jnp.float32)
            rest = jnp.dot(high, t_low, preferred_element_type=jnp.float32)
            out.append(main[:n] + (main[n:] + rest))
        return out

    def put_product(k, total):
        for g in range(xn):
            for o in range(2):
                psend[k, g, :, o * BLOCK : (o + 1) * BLOCK] = total[o][g * GROUP : (g + 1) * GROUP]

    def reduce_sends(k, same_core, target):
        waits = []
        for dg in range(xn):
            g = around(x, dg, xn)
            if k < 3:
                copy = remote(
                    psend.at[k, g], rsb.at[k, y], rs_send.at[k, dg, 0], rs_recv.at[k, y], dev(target, g, x, z)
                )
                if dg == 0 and same_core:
                    here = pltpu.make_async_copy(psend.at[k, g], rsb.at[k, y], rs_recv.at[k, y])
                    pl.when(x == y)(here.start)
                    pl.when(x != y)(copy.start)
                    waits.append(functools.partial(pl.when(x != y), copy.wait_send))
                else:
                    copy.start()
                    waits.append(copy.wait_send)
            else:
                for f in range(2):
                    part = pl.ds(f * HALF, HALF)
                    src, dst = psend.at[k, g, part, :], rsb.at[k, y, pl.ds(0, HALF), :]
                    copy = remote(src, dst, rs_send.at[k, dg, f], rs_recv.at[k, y], dev(f, g, x, z))
                    if dg == 0 and f == 1:
                        here = pltpu.make_async_copy(src, dst, rs_recv.at[k, y])
                        pl.when(x == y)(here.start)
                        pl.when(x != y)(copy.start)
                        waits.append(functools.partial(pl.when(x != y), copy.wait_send))
                    else:
                        copy.start()
                        waits.append(copy.wait_send)
        return waits

    def choices(k):
        own = oc_ref[pl.ds(pl.multiple_of(x * HALF, HALF), HALF), :]
        other = oc_ref[pl.ds(pl.multiple_of(fronts + x * HALF, HALF), HALF), :]
        return jnp.concatenate([own, other], axis=0)[:, k : k + 1]

    def weigh(total, chosen):
        first, second = total[:, 0:1], total[:, 32:33]
        both_mean = (first + second) / (2.0 * bond)
        kept_square = jnp.where(chosen == 0, first, second)
        scale = lax.rsqrt(both_mean + EPSILON)
        ratio = jnp.log(kept_square / bond + EPSILON) - jnp.log(both_mean + EPSILON)
        return scale, total[:, 64:65] + ratio

    def wait_tiles(k, same_core):
        for dy in range(xn):
            y2 = around(y, dy, xn)
            if dy == 0 and same_core:
                continue
            slot = yex.at[k, y2] if k < 3 else yexf.at[y2]
            remote(slot, slot, y_send.at[k, 0], y_recv.at[k, y2], dev(s, x, y, z)).wait_recv()

    def sum_slots(ref, rows):
        total = ref[0, rows, :]
        for j in range(1, xn):
            total = total + ref[j, rows, :]
        return total

    def reduce_group(k, rows, scale, chosen, log_sum):
        for dy in range(xn):
            j = around(y, dy, xn)
            slot = rsb.at[k, j] if k < 3 else rsb.at[k, j, pl.ds(0, HALF), :]
            remote(slot, slot, rs_send.at[k, 0, 0], rs_recv.at[k, j], dev(s, x, y, z)).wait_recv()
        total = sum_slots(rsb.at[k], pl.ds(0, rows))
        if scale is not None:
            total = total * scale
        first, second = total[:, :BLOCK], total[:, BLOCK:]
        square_first = jnp.sum(first * first, axis=1, keepdims=True)
        square_second = jnp.sum(second * second, axis=1, keepdims=True)
        kept = jnp.where(chosen == 0, first, second)
        lane = lax.broadcasted_iota(jnp.int32, (rows, LANES), 1)
        carried = jnp.where((lane >= 64) & (y == 0) & (z == 0), log_sum, 0.0)
        tile = jnp.where(lane < 32, square_first, jnp.where(lane < 64, square_second, carried))
        block = st.at[k, z, x] if k < 3 else stf.at[z, x]
        block[0] = kept[:, :LANES]
        block[1] = kept[:, LANES:]
        block[2] = tile

    def gather(k):
        waits = []
        blocks = st.at[k] if k < 3 else stf
        sub = 2 if k < 3 else 3

        def pass_on(d, z2):
            for dx in range(1, xn):
                part = blocks.at[z2, x, pl.ds(0, sub)]
                copy = remote(
                    part, part, x_send.at[k, d, dx], x_recv.at[k, z2, x], dev(s, around(x, dx, xn), y, z)
                )
                copy.start()
                waits.append(copy.wait_send)

        for d in z_order:
            copy = remote(
                blocks.at[z, x],
                blocks.at[z, x],
                z_send.at[k, d],
                z_recv.at[k, z],
                dev(s, x, y, around(z, d, zn)),
            )
            copy.start()
            waits.append(copy.wait_send)
        pass_on(0, z)
        for d in z_order:
            z2 = around(z, d, zn)
            block = blocks.at[z2, x]
            remote(block, block, z_send.at[k, d], z_recv.at[k, z2], dev(s, x, y, z)).wait_recv()
            pass_on(d, z2)
        return waits

    def wait_block(k, z2):
        blocks = st.at[k] if k < 3 else stf
        sub = 2 if k < 3 else 3
        for dx in range(1, xn):
            part = blocks.at[z2, around(x, dx, xn), pl.ds(0, sub)]
            remote(
                part, part, x_send.at[k, 0, dx], x_recv.at[k, z2, around(x, dx, xn)], dev(s, x, y, z)
            ).wait_recv()

    def tile_sends(k, same_core, targets):
        waits = []
        total = st[k, 0, x, 2]
        for j in range(1, zn):
            total = total + st[k, j, x, 2]
        ysend[k] = total
        if same_core:
            yex[k, y] = total
        for index, target in enumerate(targets):
            for dy in range(xn):
                if dy == 0 and same_core and target == 1:
                    continue
                copy = remote(
                    ysend.at[k],
                    yex.at[k, y],
                    y_send.at[k, index * xn + dy],
                    y_recv.at[k, y],
                    dev(target, x, around(y, dy, xn), z),
                )
                copy.start()
                waits.append(copy.wait_send)
        return waits

    def gathered_product(k, site):
        total = None
        for d in [0] + z_order:
            z2 = around(z, d, zn)
            wait_block(k, z2)
            lhs = jnp.concatenate(
                [jnp.concatenate([st[k, z2, g, 0], st[k, z2, g, 1]], axis=1) for g in range(xn)], axis=0
            )
            out = block_product(lhs, site, pl.multiple_of(z2 * BLOCK, BLOCK))
            total = out if total is None else [total[0] + out[0], total[1] + out[1]]
        return total

    def wait_all(waits):
        for wait in waits:
            wait()

    partner_rows = remote(x_hbm, xin.at[1], f_sem.at[0], f_sem.at[1], dev(around(s, 1, 2), x, y, z))

    @pl.when(s == 0)
    def _():
        waits = []
        own_rows.wait()
        for c in range(chunks):
            t_copy(0, c).wait()
            for b in range(t_chunk // BLOCK):
                split_rows(0, c * t_chunk + b * BLOCK)
        partner_rows.wait_recv()
        total = None
        width = BLOCK // LANES
        stride = zn * width
        for kb in range(zn):
            pieces = []
            for g in range(xn):
                for f in range(2):
                    pieces.append(
                        jnp.concatenate(
                            [
                                xin[f, pl.ds(g * HALF * stride + kb * width + c, HALF, stride=stride), :]
                                for c in range(width)
                            ],
                            axis=1,
                        )
                    )
            out = block_product(jnp.concatenate(pieces, axis=0), 0, kb * BLOCK)
            total = out if total is None else [total[0] + out[0], total[1] + out[1]]
        put_product(0, total)
        waits += reduce_sends(0, True, 0)
        for c in range(chunks):
            t_copy(1, c).wait()
            for b in range(t_chunk // BLOCK):
                split_rows(1, c * t_chunk + b * BLOCK)
        reduce_group(0, GROUP, None, choices(0), 0.0)
        waits += gather(0)
        waits += tile_sends(0, False, (1,))
        put_product(1, gathered_product(0, 1))
        waits += reduce_sends(1, False, 1)
        wait_all(waits)
        wait_tiles(2, False)

    @pl.when(s == 1)
    def _():
        waits = []
        partner_rows.start()
        waits.append(partner_rows.wait_send)
        for site in range(2):
            for c in range(chunks):
                t_copy(site, c).wait()
                for b in range(t_chunk // BLOCK):
                    split_rows(site, c * t_chunk + b * BLOCK)
        wait_tiles(0, False)
        scale, logs = weigh(sum_slots(yex.at[0], pl.ds(0, GROUP)), choices(0))
        reduce_group(1, GROUP, scale, choices(1), 0.0)
        waits += gather(1)
        waits += tile_sends(1, True, (1,))
        put_product(2, gathered_product(1, 0))
        waits += reduce_sends(2, True, 1)
        wait_tiles(1, True)
        scale, more = weigh(sum_slots(yex.at[1], pl.ds(0, GROUP)), choices(1))
        reduce_group(2, GROUP, scale, choices(2), logs + more)
        waits += gather(2)
        waits += tile_sends(2, True, (1, 0))
        put_product(3, gathered_product(2, 1))
        waits += reduce_sends(3, True, 1)
        wait_all(waits)
        wait_tiles(2, True)

    mine = oc_ref[pl.ds(pl.multiple_of(s * fronts, HALF), fronts), :]
    group_rows = pl.ds(pl.multiple_of(s * fronts + x * HALF, HALF), HALF)
    chosen = oc_ref[group_rows, :]
    scale, logs = weigh(sum_slots(yex.at[2], pl.ds(pl.multiple_of(s * HALF, HALF), HALF)), chosen[:, 2:3])
    reduce_group(3, HALF, scale, chosen[:, 3:4], logs)
    waits = gather(3)
    parts = []
    for d in [0] + z_order:
        z2 = around(z, d, zn)
        wait_block(3, z2)
        for g in range(xn):
            for c in range(2):
                column = pl.ds(pl.multiple_of(z2 * BLOCK + c * LANES, LANES), LANES)
                raw_ref[g * HALF : (g + 1) * HALF, column] = stf[z2, g, c]
    for g in range(xn):
        tile = stf[0, g, 2]
        for j in range(1, zn):
            tile = tile + stf[j, g, 2]
        parts.append(tile)
    total = jnp.concatenate(parts, axis=0)
    yexf[y] = total
    for dy in range(1, xn):
        copy = remote(
            yexf.at[y], yexf.at[y], y_send.at[3, dy], y_recv.at[3, y], dev(s, x, around(y, dy, xn), z)
        )
        copy.start()
        waits.append(copy.wait_send)
    wait_tiles(3, True)
    scale, logs = weigh(sum_slots(yexf, pl.ds(0, fronts)), mine[:, 3:4])
    lane = lax.broadcasted_iota(jnp.int32, (fronts, LANES), 1)
    aux_ref[...] = jnp.where(lane < 64, scale, logs)
    wait_all(waits)


def shards(xn, zn, initial_rows, outcomes, tensors):
    fronts, _, rows_k = initial_rows.shape
    bond = xn * rows_k
    dma = pltpu.SemaphoreType.DMA
    vmem = pl.BlockSpec(memory_space=pltpu.VMEM)
    anywhere = pl.BlockSpec(memory_space=pl.ANY)
    f32 = jnp.float32
    raw, aux = pl.pallas_call(
        functools.partial(kernel, xn, zn, float(bond)),
        out_shape=(
            jax.ShapeDtypeStruct((fronts, rows_k), f32),
            jax.ShapeDtypeStruct((fronts, LANES), f32),
        ),
        in_specs=[anywhere, vmem, anywhere],
        out_specs=(vmem, vmem),
        scratch_shapes=[
            pltpu.VMEM((2, 2, rows_k, BLOCK), f32),
            pltpu.VMEM((2, 2, rows_k, BLOCK), jnp.bfloat16),
            pltpu.VMEM((2, 2, rows_k, BLOCK), jnp.bfloat16),
            pltpu.VMEM((2, fronts * rows_k // LANES, LANES), f32),
            pltpu.VMEM((STEPS, xn, GROUP, 2 * BLOCK), f32),
            pltpu.VMEM((STEPS, xn, GROUP, 2 * BLOCK), f32),
            pltpu.VMEM((3, zn, xn, 3, GROUP, LANES), f32),
            pltpu.VMEM((zn, xn, 3, HALF, LANES), f32),
            pltpu.VMEM((3, xn, GROUP, LANES), f32),
            pltpu.VMEM((xn, fronts, LANES), f32),
            pltpu.VMEM((3, GROUP, LANES), f32),
            dma((2, max(1, rows_k // 512))),
            dma,
            dma((2,)),
            dma((STEPS, xn, 2)),
            dma((STEPS, xn)),
            dma((STEPS, zn)),
            dma((STEPS, zn)),
            dma((STEPS, zn, xn)),
            dma((STEPS, zn, xn)),
            dma((STEPS, 2 * xn)),
            dma((STEPS, xn)),
        ],
        compiler_params=pltpu.CompilerParams(
            collective_id=0, has_side_effects=True, vmem_limit_bytes=56 * 1024 * 1024
        ),
    )(initial_rows.reshape(fronts * rows_k // LANES, LANES), outcomes, tensors)
    rows = (raw * aux[:, :1])[:, None, :]
    return rows, aux[:, 64]


def solution(mesh):
    xn = mesh.shape["narrow"]
    zn = mesh.shape["wide"] // xn
    return jax.shard_map(
        functools.partial(shards, xn, zn),
        mesh=mesh,
        in_specs=(P("site", "narrow", None), P(), P("site", None, "narrow", None, "wide")),
        out_specs=(P("site", "narrow", None), P("site")),
        check_vma=False,
    )
```

```python
import functools

import jax
import jax.numpy as jnp
from jax import lax
from jax.experimental import pallas as pl
from jax.experimental.pallas import tpu as pltpu
from jax.sharding import PartitionSpec as P

MESH = pl.DeviceIdType.MESH
EPSILON = 1e-06
STEPS = 4
BLOCK = 256
GROUP = 16
HALF = 8
LANES = 128


def split_value(value):
    high = value.astype(jnp.bfloat16)
    low = (value - high.astype(jnp.float32)).astype(jnp.bfloat16)
    return high, low


def ring_distance(offset, extent):
    return min(offset, extent - offset)


def kernel(
    xn,
    zn,
    bond,
    x_hbm,
    oc_ref,
    t_hbm,
    rows_ref,
    log_ref,
    t32,
    thi,
    tlo,
    xin,
    psend,
    rsb,
    rsf,
    st,
    tl,
    stf,
    tlf,
    yex,
    yexf,
    ysend,
    tsend,
    t_sem,
    x_sem,
    rs_send,
    rs_recv,
    ag_send,
    ag_recv,
    y_send,
    y_recv,
    tl_recv,
):
    s = lax.axis_index("site")
    w = lax.axis_index("wide")
    y = lax.axis_index("narrow")
    x = lax.div(w, zn)
    z = lax.rem(w, zn)
    fronts = xn * HALF
    reach = zn // 2
    offsets = [(dz, dx) for dz in range(zn) for dx in range(xn) if dz or dx]
    offsets.sort(key=lambda o: -(ring_distance(o[0], zn) + ring_distance(o[1], xn)))

    def dev(site, xx, yy, zz):
        return (site, xx * zn + zz, yy)

    def around(value, offset, extent):
        return lax.rem(value + offset, extent)

    def remote(src, dst, send, recv, where):
        copy = pltpu.make_async_remote_copy(
            src_ref=src, dst_ref=dst, send_sem=send, recv_sem=recv, device_id=where, device_id_type=MESH
        )
        return copy

    def wait_kib(sem, kib):
        view = xin.at[0, pl.ds(0, 2 * kib), :] if kib % 8 else t32.at[0, 0, pl.ds(0, kib), :]
        pltpu.make_async_copy(view, view, sem).wait()

    rows_k = zn * BLOCK
    t_chunk = min(rows_k, 512)
    chunks = rows_k // t_chunk

    def t_copy(site, c):
        rows = pl.ds(c * t_chunk, t_chunk)
        return pltpu.make_async_copy(t_hbm.at[site, :, 0, rows, :], t32.at[site, :, rows, :], t_sem.at[site, c])

    own_rows = pltpu.make_async_copy(x_hbm, xin.at[0], x_sem.at[0])
    pl.when(s == 0)(own_rows.start)
    for site in range(2):
        for c in range(chunks):
            t_copy(site, c).start()

    barrier = pltpu.get_barrier_semaphore()
    peers = 0
    for ds in range(2):
        for dx in range(xn):
            for dy in range(xn):
                if ds or dx or dy:
                    where = dev(around(s, ds, 2), around(x, dx, xn), around(y, dy, xn), z)
                    pl.semaphore_signal(barrier, inc=1, device_id=where, device_id_type=MESH)
                    peers += 1
    for dz in range(1, zn):
        for dx in range(xn):
            where = dev(s, around(x, dx, xn), y, around(z, dz, zn))
            pl.semaphore_signal(barrier, inc=1, device_id=where, device_id_type=MESH)
            peers += 1
    pl.semaphore_wait(barrier, peers)

    def split_rows(site, start):
        for o in range(2):
            rows = pl.ds(start, BLOCK)
            high, low = split_value(t32[site, o, rows, :])
            thi[site, o, rows, :] = high
            tlo[site, o, rows, :] = low

    def split_chunk(site, c):
        t_copy(site, c).wait()
        for b in range(t_chunk // BLOCK):
            split_rows(site, c * t_chunk + b * BLOCK)

    def block_product(lhs, site, start):
        high, low = split_value(lhs)
        both = jnp.concatenate([high, low], axis=0)
        n = lhs.shape[0]
        rows = pl.ds(start, BLOCK)
        out = []
        for o in range(2):
            t_high, t_low = thi[site, o, rows, :], tlo[site, o, rows, :]
            main = jnp.dot(both, t_high, preferred_element_type=jnp.float32)
            rest = jnp.dot(high, t_low, preferred_element_type=jnp.float32)
            out.append(main[:n] + (main[n:] + rest))
        return out

    def put_product(k, total):
        for g in range(xn):
            for o in range(2):
                psend[k, g, :, o * BLOCK : (o + 1) * BLOCK] = total[o][g * GROUP : (g + 1) * GROUP]

    def reduce_sends(k, same_core, target):
        for dg in range(xn):
            g = around(x, dg, xn)
            for f in range(1 if k < 3 else 2):
                if k < 3:
                    src, dst, core = psend.at[k, g], rsb.at[k, y], target
                    here = dg == 0 and same_core
                else:
                    src, dst, core = psend.at[k, g, pl.ds(f * HALF, HALF), :], rsf.at[y], f
                    here = dg == 0 and f == 1
                copy = remote(src, dst, rs_send.at[k], rs_recv.at[k], dev(core, g, x, z))
                if here:
                    local = pltpu.make_async_copy(src, dst, rs_recv.at[k])
                    pl.when(x == y)(local.start)
                    pl.when(x != y)(copy.start)
                else:
                    copy.start()

    def end_reduce_sends(k, same_core):
        each = GROUP * 2 * BLOCK * 4 // 1024
        own = each if k < 3 else each // 2
        if same_core:
            pl.when(x == y)(lambda: wait_kib(rs_send.at[k], xn * each - own))
            pl.when(x != y)(lambda: wait_kib(rs_send.at[k], xn * each))
        else:
            wait_kib(rs_send.at[k], xn * each)

    def outcome_rows(k, rows, first_row):
        line = oc_ref[k : k + 1, :].astype(jnp.float32)
        shape = (rows, oc_ref.shape[1])
        lane = lax.broadcasted_iota(jnp.int32, shape, 1)
        row = lax.broadcasted_iota(jnp.int32, shape, 0)
        picked = jnp.where(lane == first_row(row), jnp.broadcast_to(line, shape), 0.0)
        return jnp.sum(picked, axis=1, keepdims=True) < 0.5

    def group_outcomes(k):
        return outcome_rows(
            k, GROUP, lambda row: x * HALF + jnp.where(row < HALF, row, row + (fronts - HALF))
        )

    def weigh(total, is_first):
        first, second = total[:, 0:1], total[:, 32:33]
        both_mean = (first + second) / (2.0 * bond)
        kept_square = jnp.where(is_first, first, second)
        scale = lax.rsqrt(both_mean + EPSILON)
        ratio = jnp.log(kept_square / bond + EPSILON) - jnp.log(both_mean + EPSILON)
        return scale, total[:, 64:65] + ratio

    def tree(items):
        items = list(items)
        while len(items) > 1:
            items = [sum(items[i : i + 2][1:], items[i]) for i in range(0, len(items), 2)]
        return items[0]

    def reduce_group(k, scale, is_first, log_sum):
        buffer = rsb.at[k] if k < 3 else rsf
        rows = GROUP if k < 3 else HALF
        wait_kib(rs_recv.at[k], xn * rows * 2 * BLOCK * 4 // 1024)
        total = tree(buffer[j] for j in range(xn))
        if scale is not None:
            total = total * scale
        first, second = total[:, :BLOCK], total[:, BLOCK:]
        kept = jnp.where(is_first, first, second)
        block = st.at[k, z, x] if k < 3 else stf.at[z, x]
        block[0] = kept[:, :LANES]
        block[1] = kept[:, LANES:]
        for dz, dx in offsets:
            copy = remote(
                block,
                block,
                ag_send.at[k],
                ag_recv.at[k, ring_distance(dz, zn)],
                dev(s, around(x, dx, xn), y, around(z, dz, zn)),
            )
            copy.start()
        square_first = jnp.sum(first * first, axis=1, keepdims=True)
        square_second = jnp.sum(second * second, axis=1, keepdims=True)
        lane = lax.broadcasted_iota(jnp.int32, (rows, LANES), 1)
        carried = jnp.where((lane >= 64) & (y == 0) & (z == 0), log_sum, 0.0)
        return jnp.where(lane < 32, square_first, jnp.where(lane < 64, square_second, carried))

    def end_gather_sends(k):
        each = (GROUP if k < 3 else HALF) * BLOCK * 4 // 1024
        wait_kib(ag_send.at[k], len(offsets) * each)

    def wait_blocks(k, distance):
        each = (GROUP if k < 3 else HALF) * BLOCK * 4 // 1024
        count = sum(1 for dz, dx in offsets if ring_distance(dz, zn) == distance)
        wait_kib(ag_recv.at[k, distance], count * each)

    tile_kib = GROUP * LANES * 4 // 1024

    def spread_tile(k, tile):
        tl[k, z] = tile
        for dz in range(1, zn):
            copy = remote(tl.at[k, z], tl.at[k, z], y_send.at[0], tl_recv.at[k], dev(s, x, y, around(z, dz, zn)))
            copy.start()

    def pass_tiles(k, same_core, targets):
        wait_kib(tl_recv.at[k], (zn - 1) * tile_kib)
        total = tree(tl[k, j] for j in range(zn))
        ysend[k] = total
        if same_core:
            yex[k, y] = total
        for target in targets:
            for dy in range(xn):
                if dy == 0 and same_core and target == 1:
                    continue
                where = dev(target, x, around(y, dy, xn), z)
                remote(ysend.at[k], yex.at[k, y], y_send.at[0], y_recv.at[k], where).start()

    def tile_total(k, same_core, rows):
        wait_kib(y_recv.at[k], (xn - 1 if same_core else xn) * tile_kib)
        return tree(yex[k, j, rows, :] for j in range(xn))

    def gathered_product(k, site):
        total = None
        for distance in range(reach + 1):
            wait_blocks(k, distance)
            for dz in sorted({distance, (zn - distance) % zn}):
                z2 = around(z, dz, zn)
                lhs = jnp.concatenate(
                    [jnp.concatenate([st[k, z2, g, 0], st[k, z2, g, 1]], axis=1) for g in range(xn)], axis=0
                )
                out = block_product(lhs, site, pl.multiple_of(z2 * BLOCK, BLOCK))
                total = out if total is None else [total[0] + out[0], total[1] + out[1]]
        return total

    partner_rows = remote(x_hbm, xin.at[1], x_sem.at[1], x_sem.at[2], dev(around(s, 1, 2), x, y, z))
    all_rows = pl.ds(0, GROUP)

    @pl.when(s == 0)
    def _():
        own_rows.wait()
        partner_rows.wait_recv()
        total = None
        width = BLOCK // LANES
        stride = zn * width
        for kb in range(zn):
            if kb % (t_chunk // BLOCK) == 0:
                split_chunk(0, kb * BLOCK // t_chunk)
            pieces = []
            for g in range(xn):
                for f in range(2):
                    pieces.append(
                        jnp.concatenate(
                            [
                                xin[f, pl.ds(g * HALF * stride + kb * width + c, HALF, stride=stride), :]
                                for c in range(width)
                            ],
                            axis=1,
                        )
                    )
            out = block_product(jnp.concatenate(pieces, axis=0), 0, kb * BLOCK)
            total = out if total is None else [total[0] + out[0], total[1] + out[1]]
        put_product(0, total)
        reduce_sends(0, True, 0)
        for c in range(chunks):
            split_chunk(1, c)
        spread_tile(0, reduce_group(0, None, group_outcomes(0), 0.0))
        put_product(1, gathered_product(0, 1))
        reduce_sends(1, False, 1)
        pass_tiles(0, False, (1,))
        end_reduce_sends(0, True)
        end_reduce_sends(1, False)
        end_gather_sends(0)
        wait_kib(y_send.at[0], (zn - 1 + xn) * tile_kib)
        yex[0, 0] = tile_total(2, False, all_rows)

    @pl.when(s == 1)
    def _():
        partner_rows.start()
        for site in range(2):
            for c in range(chunks):
                split_chunk(site, c)
        is_first = group_outcomes(0)
        scale, logs = weigh(tile_total(0, False, all_rows), is_first)
        is_first = group_outcomes(1)
        spread_tile(1, reduce_group(1, scale, is_first, 0.0))
        put_product(2, gathered_product(1, 0))
        reduce_sends(2, True, 1)
        pass_tiles(1, True, (1,))
        scale, more = weigh(tile_total(1, True, all_rows), is_first)
        logs = logs + more
        is_first = group_outcomes(2)
        spread_tile(2, reduce_group(2, scale, is_first, logs))
        put_product(3, gathered_product(2, 1))
        reduce_sends(3, True, 1)
        pass_tiles(2, True, (1, 0))
        partner_rows.wait_send()
        end_reduce_sends(2, True)
        end_reduce_sends(3, True)
        end_gather_sends(1)
        end_gather_sends(2)
        wait_kib(y_send.at[0], (2 * (zn - 1) + (xn - 1) + (2 * xn - 1)) * tile_kib)
        yex[0, 0] = tile_total(2, True, all_rows)

    before = yex[0, 0, pl.ds(pl.multiple_of(s * HALF, HALF), HALF), :]
    was_first = outcome_rows(2, HALF, lambda row: s * fronts + x * HALF + row)
    is_first = outcome_rows(3, HALF, lambda row: s * fronts + x * HALF + row)
    scale, logs = weigh(before, was_first)
    half_kib = HALF * LANES * 4 // 1024
    tile = reduce_group(3, scale, is_first, logs)
    tsend[...] = tile
    yexf[y] = tile
    for dy in range(1, xn):
        remote(tsend, yexf.at[y], y_send.at[1], y_recv.at[3], dev(s, x, around(y, dy, xn), z)).start()
    wait_kib(y_recv.at[3], (xn - 1) * half_kib)
    tlf[z, x] = tree(yexf[j] for j in range(xn))
    for dz, dx in offsets:
        where = dev(s, around(x, dx, xn), y, around(z, dz, zn))
        remote(tlf.at[z, x], tlf.at[z, x], y_send.at[2], tl_recv.at[3], where).start()
    is_first = outcome_rows(3, fronts, lambda row: s * fronts + row)
    for distance in range(reach + 1):
        wait_blocks(3, distance)
    wait_kib(tl_recv.at[3], len(offsets) * half_kib)
    total = jnp.concatenate([tree(tlf[j, g] for j in range(zn)) for g in range(xn)], axis=0)
    scale, logs = weigh(total, is_first)
    width = BLOCK // LANES
    stride = zn * width
    for g in range(xn):
        wide_scale = jnp.broadcast_to(scale[g * HALF : (g + 1) * HALF], (HALF, LANES))
        for j in range(zn):
            for c in range(width):
                rows_ref[pl.ds(g * HALF * stride + j * width + c, HALF, stride=stride), :] = (
                    stf[j, g, c] * wide_scale
                )
    lane = lax.broadcasted_iota(jnp.int32, (fronts, LANES), 1)
    row = lax.broadcasted_iota(jnp.int32, (fronts, LANES), 0)
    log_ref[...] = jnp.sum(jnp.where(lane == row, logs, 0.0), axis=0, keepdims=True)[:, :fronts]
    end_gather_sends(3)
    wait_kib(y_send.at[1], (xn - 1) * half_kib)
    wait_kib(y_send.at[2], len(offsets) * half_kib)


def shards(xn, zn, initial_rows, outcomes, tensors):
    fronts, _, rows_k = initial_rows.shape
    bond = xn * rows_k
    dma = pltpu.SemaphoreType.DMA
    vmem = pl.BlockSpec(memory_space=pltpu.VMEM)
    anywhere = pl.BlockSpec(memory_space=pl.ANY)
    f32 = jnp.float32
    lines = fronts * rows_k // LANES
    reach = zn // 2
    rows, logs = pl.pallas_call(
        functools.partial(kernel, xn, zn, float(bond)),
        out_shape=(
            jax.ShapeDtypeStruct((lines, LANES), f32),
            jax.ShapeDtypeStruct((1, fronts), f32),
        ),
        in_specs=[anywhere, vmem, anywhere],
        out_specs=(vmem, vmem),
        scratch_shapes=[
            pltpu.VMEM((2, 2, rows_k, BLOCK), f32),
            pltpu.VMEM((2, 2, rows_k, BLOCK), jnp.bfloat16),
            pltpu.VMEM((2, 2, rows_k, BLOCK), jnp.bfloat16),
            pltpu.VMEM((2, lines, LANES), f32),
            pltpu.VMEM((STEPS, xn, GROUP, 2 * BLOCK), f32),
            pltpu.VMEM((3, xn, GROUP, 2 * BLOCK), f32),
            pltpu.VMEM((xn, HALF, 2 * BLOCK), f32),
            pltpu.VMEM((3, zn, xn, 2, GROUP, LANES), f32),
            pltpu.VMEM((3, zn, GROUP, LANES), f32),
            pltpu.VMEM((zn, xn, 2, HALF, LANES), f32),
            pltpu.VMEM((zn, xn, HALF, LANES), f32),
            pltpu.VMEM((3, xn, GROUP, LANES), f32),
            pltpu.VMEM((xn, HALF, LANES), f32),
            pltpu.VMEM((3, GROUP, LANES), f32),
            pltpu.VMEM((HALF, LANES), f32),
            dma((2, max(1, rows_k // 512))),
            dma((3,)),
            dma((STEPS,)),
            dma((STEPS,)),
            dma((STEPS,)),
            dma((STEPS, reach + 1)),
            dma((3,)),
            dma((STEPS,)),
            dma((STEPS,)),
        ],
        compiler_params=pltpu.CompilerParams(
            collective_id=0, has_side_effects=True, vmem_limit_bytes=56 * 1024 * 1024
        ),
    )(initial_rows.reshape(lines, LANES), outcomes.T, tensors)
    return rows.reshape(fronts, 1, rows_k), logs.reshape(fronts)


def solution(mesh):
    xn = mesh.shape["narrow"]
    zn = mesh.shape["wide"] // xn
    return jax.shard_map(
        functools.partial(shards, xn, zn),
        mesh=mesh,
        in_specs=(P("site", "narrow", None), P(), P("site", None, "narrow", None, "wide")),
        out_specs=(P("site", "narrow", None), P("site")),
        check_vma=False,
    )
```

```python
import functools

import jax
import jax.numpy as jnp
from jax import lax
from jax.experimental import pallas as pl
from jax.experimental.pallas import tpu as pltpu
from jax.sharding import PartitionSpec as P

MESH = pl.DeviceIdType.MESH
EPSILON = 1e-06
STEPS = 4
BLOCK = 256
HALF = 8
LANES = 128


def split_value(value):
    high = value.astype(jnp.bfloat16)
    low = (value - high.astype(jnp.float32)).astype(jnp.bfloat16)
    return high, low


def ring_distance(offset, extent):
    return min(offset, extent - offset)


def kernel(
    xn,
    zn,
    bond,
    x_hbm,
    oc_ref,
    t_hbm,
    rows_ref,
    log_ref,
    t32,
    thi,
    tlo,
    xin,
    pfirst,
    psend,
    rsb,
    st,
    tl,
    tlf,
    yex,
    ysend,
    t_sem,
    t_send,
    t_recv,
    x_sem,
    rs_send,
    rs_recv,
    ag_send,
    ag_recv,
    y_send,
    y_recv,
    tl_recv,
):
    s = lax.axis_index("site")
    w = lax.axis_index("wide")
    y = lax.axis_index("narrow")
    x = lax.div(w, zn)
    z = lax.rem(w, zn)
    fronts = xn * HALF
    reach = zn // 2
    width = BLOCK // LANES
    stride = zn * width
    offsets = [(dz, dx) for dz in range(zn) for dx in range(xn) if dz or dx]
    offsets.sort(key=lambda o: -(ring_distance(o[0], zn) + ring_distance(o[1], xn)))
    across = sorted(range(xn), key=lambda d: -ring_distance(d, xn))

    def dev(site, xx, yy, zz):
        return (site, xx * zn + zz, yy)

    def around(value, offset, extent):
        return lax.rem(value + offset, extent)

    def remote(src, dst, send, recv, where):
        return pltpu.make_async_remote_copy(
            src_ref=src, dst_ref=dst, send_sem=send, recv_sem=recv, device_id=where, device_id_type=MESH
        )

    def wait_kib(sem, kib):
        view = xin.at[0, pl.ds(0, 2 * kib), :] if kib % 8 else t32.at[0, 0, pl.ds(0, kib), :]
        pltpu.make_async_copy(view, view, sem).wait()

    rows_k = zn * BLOCK
    t_chunk = min(rows_k, 512)
    chunks = rows_k // t_chunk
    partner = dev(around(s, 1, 2), x, y, z)

    def t_copy(local, c):
        rows = pl.ds(c * t_chunk, t_chunk)
        return pltpu.make_async_copy(
            t_hbm.at[local, :, 0, rows, :], t32.at[2 * s + local, :, rows, :], t_sem.at[local, c]
        )

    def lend(local, site, index):
        for c in range(chunks):
            rows = pl.ds(c * t_chunk, t_chunk)
            remote(
                t_hbm.at[local, :, 0, rows, :],
                t32.at[site, :, rows, :],
                t_send.at[index],
                t_recv.at[index],
                partner,
            ).start()

    def wait_site(sem):
        pltpu.make_async_copy(t32.at[0], t32.at[0], sem).wait()

    own_rows = pltpu.make_async_copy(x_hbm, xin.at[0], x_sem.at[0])
    partner_rows = remote(x_hbm, xin.at[1], x_sem.at[1], x_sem.at[2], partner)
    pl.when(s == 0)(own_rows.start)
    for local in range(2):
        for c in range(chunks):
            t_copy(local, c).start()

    barrier = pltpu.get_barrier_semaphore()
    peers = 0
    for ds in range(2):
        for dx in range(xn):
            for dy in range(xn):
                if ds or dx or dy:
                    where = dev(around(s, ds, 2), around(x, dx, xn), around(y, dy, xn), z)
                    pl.semaphore_signal(barrier, inc=1, device_id=where, device_id_type=MESH)
                    peers += 1
    for dz in range(1, zn):
        for dx in range(xn):
            where = dev(s, around(x, dx, xn), y, around(z, dz, zn))
            pl.semaphore_signal(barrier, inc=1, device_id=where, device_id_type=MESH)
            peers += 1

    def split_rows(site, start):
        for o in range(2):
            rows = pl.ds(start, BLOCK)
            high, low = split_value(t32[site, o, rows, :])
            thi[site, o, rows, :] = high
            tlo[site, o, rows, :] = low

    def split_site(site):
        for b in range(zn):
            split_rows(site, b * BLOCK)

    def block_product(lhs, site, start):
        high, low = split_value(lhs)
        both = jnp.concatenate([high, low], axis=0)
        n = lhs.shape[0]
        rows = pl.ds(start, BLOCK)
        out = []
        for o in range(2):
            t_high, t_low = thi[site, o, rows, :], tlo[site, o, rows, :]
            main = jnp.dot(both, t_high, preferred_element_type=jnp.float32)
            rest = jnp.dot(high, t_low, preferred_element_type=jnp.float32)
            out.append(main[:n] + (main[n:] + rest))
        return out

    each_part = HALF * 2 * BLOCK * 4 // 1024

    def reduce_sends(k, parts, core, maybe_here):
        for dg in across:
            g = around(x, dg, xn)
            src, dst = parts.at[g], rsb.at[k, y]
            copy = remote(src, dst, rs_send.at[k], rs_recv.at[k], dev(core, g, x, z))
            if dg == 0 and maybe_here:
                local = pltpu.make_async_copy(src, dst, rs_recv.at[k])
                pl.when(x == y)(local.start)
                pl.when(x != y)(copy.start)
            else:
                copy.start()

    def end_reduce_sends(k, count):
        pl.when(x == y)(lambda: wait_kib(rs_send.at[k], (count - 1) * each_part))
        pl.when(x != y)(lambda: wait_kib(rs_send.at[k], count * each_part))

    def outcome_rows(k, rows, first_row):
        line = oc_ref[k : k + 1, :].astype(jnp.float32)
        shape = (rows, oc_ref.shape[1])
        lane = lax.broadcasted_iota(jnp.int32, shape, 1)
        row = lax.broadcasted_iota(jnp.int32, shape, 0)
        picked = jnp.where(lane == row + first_row, jnp.broadcast_to(line, shape), 0.0)
        return jnp.sum(picked, axis=1, keepdims=True) < 0.5

    def weigh(total, is_first):
        first, second = total[:, 0:1], total[:, 32:33]
        both_mean = (first + second) / (2.0 * bond)
        kept_square = jnp.where(is_first, first, second)
        scale = lax.rsqrt(both_mean + EPSILON)
        ratio = jnp.log(kept_square / bond + EPSILON) - jnp.log(both_mean + EPSILON)
        return scale, total[:, 64:65] + ratio

    def tree(items):
        items = list(items)
        while len(items) > 1:
            items = [sum(items[i : i + 2][1:], items[i]) for i in range(0, len(items), 2)]
        return items[0]

    def reduce_group(k, scale, is_first, log_sum):
        wait_kib(rs_recv.at[k], xn * each_part)
        total = tree(rsb[k, j] for j in range(xn))
        if scale is not None:
            total = total * scale
        first, second = total[:, :BLOCK], total[:, BLOCK:]
        kept = jnp.where(is_first, first, second)
        block = st.at[k, z, x]
        block[0] = kept[:, :LANES]
        block[1] = kept[:, LANES:]
        for dz, dx in offsets:
            copy = remote(
                block,
                block,
                ag_send.at[k],
                ag_recv.at[k, ring_distance(dz, zn)],
                dev(s, around(x, dx, xn), y, around(z, dz, zn)),
            )
            copy.start()
        square_first = jnp.sum(first * first, axis=1, keepdims=True)
        square_second = jnp.sum(second * second, axis=1, keepdims=True)
        lane = lax.broadcasted_iota(jnp.int32, (HALF, LANES), 1)
        carried = jnp.where((lane >= 64) & (y == 0) & (z == 0), log_sum, 0.0)
        return jnp.where(lane < 32, square_first, jnp.where(lane < 64, square_second, carried))

    each_block = HALF * BLOCK * 4 // 1024

    def end_gather_sends(k):
        wait_kib(ag_send.at[k], len(offsets) * each_block)

    def wait_blocks(k, distance):
        count = sum(1 for dz, dx in offsets if ring_distance(dz, zn) == distance)
        wait_kib(ag_recv.at[k, distance], count * each_block)

    tile_kib = HALF * LANES * 4 // 1024

    def spread_tile(k, tile):
        tl[k, z] = tile
        for dz in range(1, zn):
            copy = remote(tl.at[k, z], tl.at[k, z], y_send.at[0], tl_recv.at[k], dev(s, x, y, around(z, dz, zn)))
            copy.start()

    def pass_tile(k, total):
        ysend[k] = total
        yex[k, y] = total
        for dy in range(1, xn):
            where = dev(s, x, around(y, dy, xn), z)
            remote(ysend.at[k], yex.at[k, y], y_send.at[1], y_recv.at[k], where).start()

    def tile_total(k):
        wait_kib(y_recv.at[k], (xn - 1) * tile_kib)
        return tree(yex[k, j] for j in range(xn))

    def gathered_product(k):
        total = None
        for distance in range(reach + 1):
            wait_blocks(k, distance)
            for dz in sorted({distance, (zn - distance) % zn}):
                z2 = around(z, dz, zn)
                lhs = jnp.concatenate(
                    [jnp.concatenate([st[k, z2, g, 0], st[k, z2, g, 1]], axis=1) for g in range(xn)], axis=0
                )
                out = block_product(lhs, k + 1, pl.multiple_of(z2 * BLOCK, BLOCK))
                total = out if total is None else [total[0] + out[0], total[1] + out[1]]
        for g in range(xn):
            for o in range(2):
                psend[k, g, :, o * BLOCK : (o + 1) * BLOCK] = total[o][g * HALF : (g + 1) * HALF]

    @pl.when(s == 0)
    def _():
        own_rows.wait()
        for c in range(chunks):
            t_copy(0, c).wait()
            for b in range(t_chunk // BLOCK):
                split_rows(0, c * t_chunk + b * BLOCK)

    pl.semaphore_wait(barrier, peers)

    @pl.when(s == 0)
    def _():
        partner_rows.wait_recv()
        total = None
        for kb in range(zn):
            pieces = [
                jnp.concatenate(
                    [
                        xin[f, pl.ds(g * HALF * stride + kb * width + c, HALF, stride=stride), :]
                        for c in range(width)
                    ],
                    axis=1,
                )
                for f in range(2)
                for g in range(xn)
            ]
            out = block_product(jnp.concatenate(pieces, axis=0), 0, kb * BLOCK)
            total = out if total is None else [total[0] + out[0], total[1] + out[1]]
        for f in range(2):
            for g in range(xn):
                row = (f * xn + g) * HALF
                for o in range(2):
                    pfirst[f, g, :, o * BLOCK : (o + 1) * BLOCK] = total[o][row : row + HALF]
        reduce_sends(0, pfirst.at[1], 1, False)
        reduce_sends(0, pfirst.at[0], 0, True)
        lend(1, 1, 0)
        for c in range(chunks):
            t_copy(1, c).wait()
        split_site(1)

    @pl.when(s == 1)
    def _():
        partner_rows.start()
        lend(0, 2, 1)
        for local in range(2):
            for c in range(chunks):
                t_copy(local, c).wait()
            split_site(2 + local)

    own_first = s * fronts + x * HALF
    is_first = outcome_rows(0, HALF, own_first)
    spread_tile(0, reduce_group(0, None, is_first, 0.0))

    @pl.when(s == 1)
    def _():
        lend(1, 3, 2)
        wait_site(t_recv.at[0])
        split_site(1)

    logs = jnp.zeros((HALF, 1), jnp.float32)
    for k in range(1, STEPS):
        gathered_product(k - 1)
        reduce_sends(k, psend.at[k - 1], s, True)
        wait_kib(tl_recv.at[k - 1], (zn - 1) * tile_kib)
        pass_tile(k - 1, tree(tl[k - 1, j] for j in range(zn)))
        if k < STEPS - 1:

            @pl.when(s == 0)
            def _():
                wait_site(t_recv.at[k])
                split_site(k + 1)

        was_first, is_first = is_first, outcome_rows(k, HALF, own_first)
        scale, more = weigh(tile_total(k - 1), was_first)
        logs = logs + more
        tile = reduce_group(k, scale, is_first, logs if k == STEPS - 1 else 0.0)
        if k < STEPS - 1:
            spread_tile(k, tile)

    last = STEPS - 1
    pass_tile(last, tile)
    tlf[z, x] = tile_total(last)
    for dz, dx in offsets:
        where = dev(s, around(x, dx, xn), y, around(z, dz, zn))
        remote(tlf.at[z, x], tlf.at[z, x], y_send.at[2], tl_recv.at[last], where).start()
    is_first = outcome_rows(last, fronts, s * fronts)
    for distance in range(reach + 1):
        wait_blocks(last, distance)
    wait_kib(tl_recv.at[last], len(offsets) * tile_kib)
    total = jnp.concatenate([tree(tlf[j, g] for j in range(zn)) for g in range(xn)], axis=0)
    scale, logs = weigh(total, is_first)
    for g in range(xn):
        wide_scale = jnp.broadcast_to(scale[g * HALF : (g + 1) * HALF], (HALF, LANES))
        for j in range(zn):
            for c in range(width):
                rows_ref[pl.ds(g * HALF * stride + j * width + c, HALF, stride=stride), :] = (
                    st[last, j, g, c] * wide_scale
                )
    lane = lax.broadcasted_iota(jnp.int32, (fronts, LANES), 1)
    row = lax.broadcasted_iota(jnp.int32, (fronts, LANES), 0)
    log_ref[...] = jnp.sum(jnp.where(lane == row, logs, 0.0), axis=0, keepdims=True)[:, :fronts]

    @pl.when(s == 0)
    def _():
        end_reduce_sends(0, 2 * xn)
        wait_site(t_send.at[0])

    @pl.when(s == 1)
    def _():
        partner_rows.wait_send()
        wait_site(t_send.at[1])
        wait_site(t_send.at[2])

    for k in range(STEPS):
        if k:
            end_reduce_sends(k, xn)
        end_gather_sends(k)
    wait_kib(y_send.at[0], (STEPS - 1) * (zn - 1) * tile_kib)
    wait_kib(y_send.at[1], STEPS * (xn - 1) * tile_kib)
    wait_kib(y_send.at[2], len(offsets) * tile_kib)


def shards(xn, zn, initial_rows, outcomes, tensors):
    fronts, _, rows_k = initial_rows.shape
    bond = xn * rows_k
    dma = pltpu.SemaphoreType.DMA
    vmem = pl.BlockSpec(memory_space=pltpu.VMEM)
    anywhere = pl.BlockSpec(memory_space=pl.ANY)
    f32 = jnp.float32
    lines = fronts * rows_k // LANES
    reach = zn // 2
    rows, logs = pl.pallas_call(
        functools.partial(kernel, xn, zn, float(bond)),
        out_shape=(
            jax.ShapeDtypeStruct((lines, LANES), f32),
            jax.ShapeDtypeStruct((1, fronts), f32),
        ),
        in_specs=[anywhere, vmem, anywhere],
        out_specs=(vmem, vmem),
        scratch_shapes=[
            pltpu.VMEM((STEPS, 2, rows_k, BLOCK), f32),
            pltpu.VMEM((STEPS, 2, rows_k, BLOCK), jnp.bfloat16),
            pltpu.VMEM((STEPS, 2, rows_k, BLOCK), jnp.bfloat16),
            pltpu.VMEM((2, lines, LANES), f32),
            pltpu.VMEM((2, xn, HALF, 2 * BLOCK), f32),
            pltpu.VMEM((STEPS - 1, xn, HALF, 2 * BLOCK), f32),
            pltpu.VMEM((STEPS, xn, HALF, 2 * BLOCK), f32),
            pltpu.VMEM((STEPS, zn, xn, 2, HALF, LANES), f32),
            pltpu.VMEM((STEPS - 1, zn, HALF, LANES), f32),
            pltpu.VMEM((zn, xn, HALF, LANES), f32),
            pltpu.VMEM((STEPS, xn, HALF, LANES), f32),
            pltpu.VMEM((STEPS, HALF, LANES), f32),
            dma((2, max(1, rows_k // 512))),
            dma((3,)),
            dma((3,)),
            dma((3,)),
            dma((STEPS,)),
            dma((STEPS,)),
            dma((STEPS,)),
            dma((STEPS, reach + 1)),
            dma((3,)),
            dma((STEPS,)),
            dma((STEPS,)),
        ],
        compiler_params=pltpu.CompilerParams(
            collective_id=0, has_side_effects=True, vmem_limit_bytes=56 * 1024 * 1024
        ),
    )(initial_rows.reshape(lines, LANES), outcomes.T, tensors)
    return rows.reshape(fronts, 1, rows_k), logs.reshape(fronts)


def solution(mesh):
    xn = mesh.shape["narrow"]
    zn = mesh.shape["wide"] // xn
    return jax.shard_map(
        functools.partial(shards, xn, zn),
        mesh=mesh,
        in_specs=(P("site", "narrow", None), P(), P("site", None, "narrow", None, "wide")),
        out_specs=(P("site", "narrow", None), P("site")),
        check_vma=False,
    )
```

```python
import functools

import jax
import jax.numpy as jnp
from jax import lax
from jax.experimental import pallas as pl
from jax.experimental.pallas import tpu as pltpu
from jax.sharding import PartitionSpec as P

MESH = pl.DeviceIdType.MESH
EPSILON = 1e-06
STEPS = 4
RELAYED = (1,)
BLOCK = 256
HALF = 8
LANES = 128


def split_value(value):
    high = value.astype(jnp.bfloat16)
    low = (value - high.astype(jnp.float32)).astype(jnp.bfloat16)
    return high, low


def ring_distance(offset, extent):
    return min(offset, extent - offset)


def kernel(
    xn,
    zn,
    bond,
    x_hbm,
    oc_ref,
    t_hbm,
    rows_ref,
    log_ref,
    t32,
    thi,
    tlo,
    xin,
    pfirst,
    psend,
    rsb,
    st,
    tl,
    tlf,
    yex,
    ysend,
    t_sem,
    t_send,
    t_recv,
    x_sem,
    rs_send,
    rs_recv,
    ag_send,
    ag_recv,
    y_send,
    y_recv,
    tl_recv,
    relay_recv,
):
    s = lax.axis_index("site")
    w = lax.axis_index("wide")
    y = lax.axis_index("narrow")
    x = lax.div(w, zn)
    z = lax.rem(w, zn)
    fronts = xn * HALF
    reach = zn // 2
    width = BLOCK // LANES
    stride = zn * width
    offsets = [(dz, dx) for dz in range(zn) for dx in range(xn) if dz or dx]
    offsets.sort(key=lambda o: -(ring_distance(o[0], zn) + ring_distance(o[1], xn)))
    across = sorted(range(xn), key=lambda d: -ring_distance(d, xn))

    def dev(site, xx, yy, zz):
        return (site, xx * zn + zz, yy)

    def around(value, offset, extent):
        return lax.rem(value + offset, extent)

    def remote(src, dst, send, recv, where):
        return pltpu.make_async_remote_copy(
            src_ref=src, dst_ref=dst, send_sem=send, recv_sem=recv, device_id=where, device_id_type=MESH
        )

    def wait_kib(sem, kib):
        view = xin.at[0, pl.ds(0, 2 * kib), :] if kib % 8 else t32.at[0, 0, pl.ds(0, kib), :]
        pltpu.make_async_copy(view, view, sem).wait()

    rows_k = zn * BLOCK
    t_chunk = min(rows_k, 512)
    chunks = rows_k // t_chunk
    partner = dev(around(s, 1, 2), x, y, z)

    def t_copy(local, c):
        rows = pl.ds(c * t_chunk, t_chunk)
        return pltpu.make_async_copy(
            t_hbm.at[local, :, 0, rows, :], t32.at[2 * s + local, :, rows, :], t_sem.at[local, c]
        )

    def lend(local, site, index):
        for c in range(chunks):
            rows = pl.ds(c * t_chunk, t_chunk)
            remote(
                t_hbm.at[local, :, 0, rows, :],
                t32.at[site, :, rows, :],
                t_send.at[index],
                t_recv.at[index],
                partner,
            ).start()

    def wait_site(sem):
        pltpu.make_async_copy(t32.at[0], t32.at[0], sem).wait()

    own_rows = pltpu.make_async_copy(x_hbm, xin.at[0], x_sem.at[0])
    partner_rows = remote(xin.at[0], xin.at[1], x_sem.at[1], x_sem.at[2], partner)
    own_rows.start()
    for local in range(2):
        for c in range(chunks):
            t_copy(local, c).start()

    barrier = pltpu.get_barrier_semaphore()
    peers = 0
    for ds in range(2):
        for dx in range(xn):
            for dy in range(xn):
                if ds or dx or dy:
                    where = dev(around(s, ds, 2), around(x, dx, xn), around(y, dy, xn), z)
                    pl.semaphore_signal(barrier, inc=1, device_id=where, device_id_type=MESH)
                    peers += 1
    for dz in range(1, zn):
        for dx in range(xn):
            where = dev(s, around(x, dx, xn), y, around(z, dz, zn))
            pl.semaphore_signal(barrier, inc=1, device_id=where, device_id_type=MESH)
            peers += 1

    def split_rows(site, start):
        for o in range(2):
            rows = pl.ds(start, BLOCK)
            high, low = split_value(t32[site, o, rows, :])
            thi[site, o, rows, :] = high
            tlo[site, o, rows, :] = low

    def split_site(site):
        for b in range(zn):
            split_rows(site, b * BLOCK)

    def block_product(lhs, site, starts):
        high, low = split_value(lhs)
        both = jnp.concatenate([high, low], axis=0)
        n = lhs.shape[0]
        out = []
        for o in range(2):
            t_high, t_low = (
                jnp.concatenate([half[site, o, pl.ds(start, BLOCK), :] for start in starts], axis=0)
                for half in (thi, tlo)
            )
            main = jnp.dot(both, t_high, preferred_element_type=jnp.float32)
            rest = jnp.dot(high, t_low, preferred_element_type=jnp.float32)
            out.append(main[:n] + (main[n:] + rest))
        return out

    each_part = HALF * 2 * BLOCK * 4 // 1024

    def reduce_sends(k, parts, core, maybe_here):
        for dg in across:
            g = around(x, dg, xn)
            src, dst = parts.at[g], rsb.at[k, y]
            copy = remote(src, dst, rs_send.at[k], rs_recv.at[k], dev(core, g, x, z))
            if dg == 0 and maybe_here:
                local = pltpu.make_async_copy(src, dst, rs_recv.at[k])
                pl.when(x == y)(local.start)
                pl.when(x != y)(copy.start)
            else:
                copy.start()

    def end_reduce_sends(k, count):
        pl.when(x == y)(lambda: wait_kib(rs_send.at[k], (count - 1) * each_part))
        pl.when(x != y)(lambda: wait_kib(rs_send.at[k], count * each_part))

    def outcome_rows(k, rows, first_row):
        line = oc_ref[k : k + 1, :].astype(jnp.float32)
        shape = (rows, oc_ref.shape[1])
        lane = lax.broadcasted_iota(jnp.int32, shape, 1)
        row = lax.broadcasted_iota(jnp.int32, shape, 0)
        picked = jnp.where(lane == row + first_row, jnp.broadcast_to(line, shape), 0.0)
        return jnp.sum(picked, axis=1, keepdims=True) < 0.5

    def weigh(total, is_first):
        first, second = total[:, 0:1], total[:, 32:33]
        both_mean = (first + second) / (2.0 * bond)
        kept_square = jnp.where(is_first, first, second)
        scale = lax.rsqrt(both_mean + EPSILON)
        ratio = jnp.log(kept_square / bond + EPSILON) - jnp.log(both_mean + EPSILON)
        return scale, total[:, 64:65] + ratio

    def tree(items):
        items = list(items)
        while len(items) > 1:
            items = [sum(items[i : i + 2][1:], items[i]) for i in range(0, len(items), 2)]
        return items[0]

    def reduce_group(k, scale, is_first, log_sum):
        wait_kib(rs_recv.at[k], xn * each_part)
        total = tree(rsb[k, j] for j in range(xn))
        if scale is not None:
            total = total * scale
        first, second = total[:, :BLOCK], total[:, BLOCK:]
        kept = jnp.where(is_first, first, second)
        block = st.at[k, z, x]
        block[0] = kept[:, :LANES]
        block[1] = kept[:, LANES:]
        for dz, dx in sorted(offsets, key=lambda o: ring_distance(o[0], zn) not in RELAYED):
            distance = ring_distance(dz, zn)
            if distance in RELAYED:
                if dx:
                    continue
                arrived = relay_recv.at[k, distance]
            else:
                arrived = ag_recv.at[k, distance]
            where = dev(s, around(x, dx, xn), y, around(z, dz, zn))
            remote(block, block, ag_send.at[k], arrived, where).start()
        square_first = jnp.sum(first * first, axis=1, keepdims=True)
        square_second = jnp.sum(second * second, axis=1, keepdims=True)
        lane = lax.broadcasted_iota(jnp.int32, (HALF, LANES), 1)
        carried = jnp.where((lane >= 64) & (y == 0) & (z == 0), log_sum, 0.0)
        return jnp.where(lane < 32, square_first, jnp.where(lane < 64, square_second, carried))

    each_block = HALF * BLOCK * 4 // 1024

    def end_gather_sends(k):
        wait_kib(ag_send.at[k], len(offsets) * each_block)

    def relay(k, low, high):
        for distance in range(low, high + 1):
            if distance in RELAYED:
                offset_pair = sorted({distance, zn - distance})
                wait_kib(relay_recv.at[k, distance], len(offset_pair) * each_block)
                for dz in offset_pair:
                    block = st.at[k, around(z, dz, zn), x]
                    for dx in across[:-1]:
                        where = dev(s, around(x, dx, xn), y, z)
                        remote(block, block, ag_send.at[k], ag_recv.at[k, distance], where).start()

    def wait_blocks(k, distance):
        count = sum(1 for dz, dx in offsets if ring_distance(dz, zn) == distance)
        if distance in RELAYED:
            count = count * (xn - 1) // xn
        wait_kib(ag_recv.at[k, distance], count * each_block)

    tile_kib = HALF * LANES * 4 // 1024

    def spread_tile(k, tile):
        tl[k, z] = tile
        for dz in range(1, zn):
            copy = remote(tl.at[k, z], tl.at[k, z], y_send.at[0], tl_recv.at[k], dev(s, x, y, around(z, dz, zn)))
            copy.start()

    def pass_tile(k, total):
        ysend[k] = total
        yex[k, y] = total
        for dy in range(1, xn):
            where = dev(s, x, around(y, dy, xn), z)
            remote(ysend.at[k], yex.at[k, y], y_send.at[1], y_recv.at[k], where).start()

    def tile_total(k):
        wait_kib(y_recv.at[k], (xn - 1) * tile_kib)
        return tree(yex[k, j] for j in range(xn))

    def gathered_product(k):
        total = None
        for distance in range(reach + 1):
            wait_blocks(k, distance)
            places = [around(z, dz, zn) for dz in sorted({distance, (zn - distance) % zn})]
            lhs = jnp.concatenate(
                [
                    jnp.concatenate([st[k, z2, g, c] for z2 in places for c in range(width)], axis=1)
                    for g in range(xn)
                ],
                axis=0,
            )
            out = block_product(lhs, k + 1, [pl.multiple_of(z2 * BLOCK, BLOCK) for z2 in places])
            total = out if total is None else [total[0] + out[0], total[1] + out[1]]
        for g in range(xn):
            for o in range(2):
                psend[k, g, :, o * BLOCK : (o + 1) * BLOCK] = total[o][g * HALF : (g + 1) * HALF]

    @pl.when(s == 0)
    def _():
        own_rows.wait()
        for c in range(chunks):
            t_copy(0, c).wait()
            for b in range(t_chunk // BLOCK):
                split_rows(0, c * t_chunk + b * BLOCK)

    pl.semaphore_wait(barrier, peers)

    @pl.when(s == 0)
    def _():
        partner_rows.wait_recv()
        total = None
        for kb in range(zn):
            pieces = [
                jnp.concatenate(
                    [
                        xin[f, pl.ds(g * HALF * stride + kb * width + c, HALF, stride=stride), :]
                        for c in range(width)
                    ],
                    axis=1,
                )
                for f in range(2)
                for g in range(xn)
            ]
            out = block_product(jnp.concatenate(pieces, axis=0), 0, [kb * BLOCK])
            total = out if total is None else [total[0] + out[0], total[1] + out[1]]
        for f in range(2):
            for g in range(xn):
                row = (f * xn + g) * HALF
                for o in range(2):
                    pfirst[f, g, :, o * BLOCK : (o + 1) * BLOCK] = total[o][row : row + HALF]
        reduce_sends(0, pfirst.at[1], 1, False)
        reduce_sends(0, pfirst.at[0], 0, True)
        lend(1, 1, 0)
        for c in range(chunks):
            t_copy(1, c).wait()
        split_site(1)

    @pl.when(s == 1)
    def _():
        own_rows.wait()
        partner_rows.start()
        lend(0, 2, 1)
        for local in range(2):
            for c in range(chunks):
                t_copy(local, c).wait()
            split_site(2 + local)

    own_first = s * fronts + x * HALF
    is_first = outcome_rows(0, HALF, own_first)
    spread_tile(0, reduce_group(0, None, is_first, 0.0))
    relay(0, 1, reach)

    @pl.when(s == 1)
    def _():
        lend(1, 3, 2)
        wait_site(t_recv.at[0])
        split_site(1)

    logs = jnp.zeros((HALF, 1), jnp.float32)
    for k in range(1, STEPS):
        gathered_product(k - 1)
        reduce_sends(k, psend.at[k - 1], s, True)
        wait_kib(tl_recv.at[k - 1], (zn - 1) * tile_kib)
        pass_tile(k - 1, tree(tl[k - 1, j] for j in range(zn)))
        if k < STEPS - 1:

            @pl.when(s == 0)
            def _():
                wait_site(t_recv.at[k])
                split_site(k + 1)

        was_first, is_first = is_first, outcome_rows(k, HALF, own_first)
        scale, more = weigh(tile_total(k - 1), was_first)
        logs = logs + more
        tile = reduce_group(k, scale, is_first, logs if k == STEPS - 1 else 0.0)
        if k < STEPS - 1:
            spread_tile(k, tile)
            relay(k, 1, reach)

    last = STEPS - 1
    pass_tile(last, tile)
    relay(last, 1, 1)
    tlf[z, x] = tile_total(last)
    for dz, dx in offsets:
        where = dev(s, around(x, dx, xn), y, around(z, dz, zn))
        remote(tlf.at[z, x], tlf.at[z, x], y_send.at[2], tl_recv.at[last], where).start()
    relay(last, 2, reach)
    is_first = outcome_rows(last, fronts, s * fronts)
    for distance in range(reach + 1):
        wait_blocks(last, distance)
    wait_kib(tl_recv.at[last], len(offsets) * tile_kib)
    total = jnp.concatenate([tree(tlf[j, g] for j in range(zn)) for g in range(xn)], axis=0)
    scale, logs = weigh(total, is_first)
    for g in range(xn):
        wide_scale = jnp.broadcast_to(scale[g * HALF : (g + 1) * HALF], (HALF, LANES))
        for j in range(zn):
            for c in range(width):
                rows_ref[pl.ds(g * HALF * stride + j * width + c, HALF, stride=stride), :] = (
                    st[last, j, g, c] * wide_scale
                )
    lane = lax.broadcasted_iota(jnp.int32, (fronts, LANES), 1)
    row = lax.broadcasted_iota(jnp.int32, (fronts, LANES), 0)
    log_ref[...] = jnp.sum(jnp.where(lane == row, logs, 0.0), axis=0, keepdims=True)[:, :fronts]

    @pl.when(s == 0)
    def _():
        end_reduce_sends(0, 2 * xn)
        wait_site(t_send.at[0])

    @pl.when(s == 1)
    def _():
        partner_rows.wait_send()
        wait_site(t_send.at[1])
        wait_site(t_send.at[2])

    for k in range(STEPS):
        if k:
            end_reduce_sends(k, xn)
        end_gather_sends(k)
    wait_kib(y_send.at[0], (STEPS - 1) * (zn - 1) * tile_kib)
    wait_kib(y_send.at[1], STEPS * (xn - 1) * tile_kib)
    wait_kib(y_send.at[2], len(offsets) * tile_kib)


def deliver(rows_ref, log_ref, rows_out, log_out, sem):
    copies = (
        pltpu.make_async_copy(rows_ref, rows_out, sem.at[0]),
        pltpu.make_async_copy(log_ref, log_out, sem.at[1]),
    )
    for copy in copies:
        copy.start()
    for copy in copies:
        copy.wait()


def shards(xn, zn, initial_rows, outcomes, tensors):
    fronts, _, rows_k = initial_rows.shape
    bond = xn * rows_k
    dma = pltpu.SemaphoreType.DMA
    vmem = pl.BlockSpec(memory_space=pltpu.VMEM)
    anywhere = pl.BlockSpec(memory_space=pl.ANY)
    f32 = jnp.float32
    lines = fronts * rows_k // LANES
    reach = zn // 2
    rows, logs = pl.pallas_call(
        functools.partial(kernel, xn, zn, float(bond)),
        out_shape=(
            pltpu.VMEM((lines, LANES), f32),
            pltpu.VMEM((1, fronts), f32),
        ),
        in_specs=[anywhere, vmem, anywhere],
        out_specs=(vmem, vmem),
        scratch_shapes=[
            pltpu.VMEM((STEPS, 2, rows_k, BLOCK), f32),
            pltpu.VMEM((STEPS, 2, rows_k, BLOCK), jnp.bfloat16),
            pltpu.VMEM((STEPS, 2, rows_k, BLOCK), jnp.bfloat16),
            pltpu.VMEM((2, lines, LANES), f32),
            pltpu.VMEM((2, xn, HALF, 2 * BLOCK), f32),
            pltpu.VMEM((STEPS - 1, xn, HALF, 2 * BLOCK), f32),
            pltpu.VMEM((STEPS, xn, HALF, 2 * BLOCK), f32),
            pltpu.VMEM((STEPS, zn, xn, 2, HALF, LANES), f32),
            pltpu.VMEM((STEPS - 1, zn, HALF, LANES), f32),
            pltpu.VMEM((zn, xn, HALF, LANES), f32),
            pltpu.VMEM((STEPS, xn, HALF, LANES), f32),
            pltpu.VMEM((STEPS, HALF, LANES), f32),
            dma((2, max(1, rows_k // 512))),
            dma((3,)),
            dma((3,)),
            dma((3,)),
            dma((STEPS,)),
            dma((STEPS,)),
            dma((STEPS,)),
            dma((STEPS, reach + 1)),
            dma((3,)),
            dma((STEPS,)),
            dma((STEPS,)),
            dma((STEPS, reach + 1)),
        ],
        compiler_params=pltpu.CompilerParams(
            collective_id=0, has_side_effects=True, vmem_limit_bytes=56 * 1024 * 1024
        ),
    )(initial_rows.reshape(lines, LANES), outcomes.T, tensors)
    rows, logs = pl.pallas_call(
        deliver,
        out_shape=(
            jax.ShapeDtypeStruct((lines, LANES), f32),
            jax.ShapeDtypeStruct((1, fronts), f32),
        ),
        in_specs=[vmem, vmem],
        out_specs=(anywhere, anywhere),
        scratch_shapes=[dma((2,))],
    )(pltpu.with_memory_space_constraint(rows, pltpu.VMEM), pltpu.with_memory_space_constraint(logs, pltpu.VMEM))
    return rows.reshape(fronts, 1, rows_k), logs.reshape(fronts)


def solution(mesh):
    xn = mesh.shape["narrow"]
    zn = mesh.shape["wide"] // xn
    return jax.shard_map(
        functools.partial(shards, xn, zn),
        mesh=mesh,
        in_specs=(P("site", "narrow", None), P(), P("site", None, "narrow", None, "wide")),
        out_specs=(P("site", "narrow", None), P("site")),
        check_vma=False,
    )
```

```python
import functools

import jax
import jax.numpy as jnp
from jax import lax
from jax.experimental import pallas as pl
from jax.experimental.pallas import tpu as pltpu
from jax.sharding import PartitionSpec as P

MESH = pl.DeviceIdType.MESH
EPSILON = 1e-06
STEPS = 4
RELAYED = (1,)
BLOCK = 256
HALF = 8
LANES = 128


def split_value(value):
    high = value.astype(jnp.bfloat16)
    low = (value - high.astype(jnp.float32)).astype(jnp.bfloat16)
    return high, low


def ring_distance(offset, extent):
    return min(offset, extent - offset)


def kernel(
    xn,
    zn,
    bond,
    x_hbm,
    oc_ref,
    t_hbm,
    rows_ref,
    log_ref,
    t32,
    thi,
    tlo,
    xin,
    pfirst,
    psend,
    rsb,
    st,
    tl,
    tlf,
    yex,
    ysend,
    t_sem,
    t_send,
    t_recv,
    x_sem,
    rs_send,
    rs_recv,
    ag_send,
    ag_recv,
    y_send,
    y_recv,
    tl_recv,
    relay_recv,
):
    s = lax.axis_index("site")
    w = lax.axis_index("wide")
    y = lax.axis_index("narrow")
    x = lax.div(w, zn)
    z = lax.rem(w, zn)
    fronts = xn * HALF
    reach = zn // 2
    width = BLOCK // LANES
    stride = zn * width
    offsets = [(dz, dx) for dz in range(zn) for dx in range(xn) if dz or dx]
    offsets.sort(key=lambda o: (-(ring_distance(o[0], zn) + 2 * ring_distance(o[1], xn)), o[0]))
    across = sorted(range(xn), key=lambda d: -ring_distance(d, xn))

    def dev(site, xx, yy, zz):
        return (site, xx * zn + zz, yy)

    def around(value, offset, extent):
        return lax.rem(value + offset, extent)

    def remote(src, dst, send, recv, where):
        return pltpu.make_async_remote_copy(
            src_ref=src, dst_ref=dst, send_sem=send, recv_sem=recv, device_id=where, device_id_type=MESH
        )

    def wait_kib(sem, kib):
        view = xin.at[0, pl.ds(0, 2 * kib), :] if kib % 8 else t32.at[0, 0, pl.ds(0, kib), :]
        pltpu.make_async_copy(view, view, sem).wait()

    rows_k = zn * BLOCK
    t_chunk = min(rows_k, 512)
    chunks = rows_k // t_chunk
    partner = dev(around(s, 1, 2), x, y, z)

    def t_copy(local, c):
        rows = pl.ds(c * t_chunk, t_chunk)
        return pltpu.make_async_copy(
            t_hbm.at[local, :, 0, rows, :], t32.at[2 * s + local, :, rows, :], t_sem.at[local, c]
        )

    def lend(local, site, index):
        for c in range(chunks):
            rows = pl.ds(c * t_chunk, t_chunk)
            remote(
                t_hbm.at[local, :, 0, rows, :],
                t32.at[site, :, rows, :],
                t_send.at[index],
                t_recv.at[index],
                partner,
            ).start()

    def wait_site(sem):
        pltpu.make_async_copy(t32.at[0], t32.at[0], sem).wait()

    own_rows = pltpu.make_async_copy(x_hbm, xin.at[0], x_sem.at[0])
    partner_rows = remote(xin.at[0], xin.at[1], x_sem.at[1], x_sem.at[2], partner)
    own_rows.start()
    for local in range(2):
        for c in range(chunks):
            t_copy(local, c).start()

    barrier = pltpu.get_barrier_semaphore()
    peers = 0
    for ds in range(2):
        for dx in range(xn):
            for dy in range(xn):
                if ds or dx or dy:
                    where = dev(around(s, ds, 2), around(x, dx, xn), around(y, dy, xn), z)
                    pl.semaphore_signal(barrier, inc=1, device_id=where, device_id_type=MESH)
                    peers += 1
    for dz in range(1, zn):
        for dx in range(xn):
            where = dev(s, around(x, dx, xn), y, around(z, dz, zn))
            pl.semaphore_signal(barrier, inc=1, device_id=where, device_id_type=MESH)
            peers += 1

    def split_rows(site, start):
        for o in range(2):
            rows = pl.ds(start, BLOCK)
            high, low = split_value(t32[site, o, rows, :])
            thi[site, o, rows, :] = high
            tlo[site, o, rows, :] = low

    def split_site(site):
        for b in range(zn):
            split_rows(site, b * BLOCK)

    def block_product(lhs, site, starts):
        high, low = split_value(lhs)
        both = jnp.concatenate([high, low], axis=0)
        n = lhs.shape[0]
        out = []
        for o in range(2):
            t_high, t_low = (
                jnp.concatenate([half[site, o, pl.ds(start, BLOCK), :] for start in starts], axis=0)
                for half in (thi, tlo)
            )
            main = jnp.dot(both, t_high, preferred_element_type=jnp.float32)
            rest = jnp.dot(high, t_low, preferred_element_type=jnp.float32)
            out.append(main[:n] + (main[n:] + rest))
        return out

    each_part = HALF * 2 * BLOCK * 4 // 1024

    def reduce_sends(k, parts, core, maybe_here):
        for dg in across:
            g = around(x, dg, xn)
            src, dst = parts.at[g], rsb.at[k, y]
            copy = remote(src, dst, rs_send.at[k], rs_recv.at[k], dev(core, g, x, z))
            if dg == 0 and maybe_here:
                local = pltpu.make_async_copy(src, dst, rs_recv.at[k])
                pl.when(x == y)(local.start)
                pl.when(x != y)(copy.start)
            else:
                copy.start()

    def end_reduce_sends(k, count):
        pl.when(x == y)(lambda: wait_kib(rs_send.at[k], (count - 1) * each_part))
        pl.when(x != y)(lambda: wait_kib(rs_send.at[k], count * each_part))

    def outcome_rows(k, rows, first_row):
        line = oc_ref[k : k + 1, :].astype(jnp.float32)
        shape = (rows, oc_ref.shape[1])
        lane = lax.broadcasted_iota(jnp.int32, shape, 1)
        row = lax.broadcasted_iota(jnp.int32, shape, 0)
        picked = jnp.where(lane == row + first_row, jnp.broadcast_to(line, shape), 0.0)
        return jnp.sum(picked, axis=1, keepdims=True) < 0.5

    def weigh(total, is_first):
        first, second = total[:, 0:1], total[:, 32:33]
        both_mean = (first + second) / (2.0 * bond)
        kept_square = jnp.where(is_first, first, second)
        scale = lax.rsqrt(both_mean + EPSILON)
        ratio = jnp.log(kept_square / bond + EPSILON) - jnp.log(both_mean + EPSILON)
        return scale, total[:, 64:65] + ratio

    def tree(items):
        items = list(items)
        while len(items) > 1:
            items = [sum(items[i : i + 2][1:], items[i]) for i in range(0, len(items), 2)]
        return items[0]

    def reduce_group(k, scale, is_first, log_sum):
        wait_kib(rs_recv.at[k], xn * each_part)
        total = tree(rsb[k, j] for j in range(xn))
        if scale is not None:
            total = total * scale
        first, second = total[:, :BLOCK], total[:, BLOCK:]
        kept = jnp.where(is_first, first, second)
        block = st.at[k, z, x]
        block[0] = kept[:, :LANES]
        block[1] = kept[:, LANES:]
        for dz, dx in sorted(offsets, key=lambda o: ring_distance(o[0], zn) not in RELAYED):
            distance = ring_distance(dz, zn)
            if distance in RELAYED:
                if dx:
                    continue
                arrived = relay_recv.at[k]
            else:
                arrived = ag_recv.at[k, distance]
            where = dev(s, around(x, dx, xn), y, around(z, dz, zn))
            remote(block, block, ag_send.at[k], arrived, where).start()
        square_first = jnp.sum(first * first, axis=1, keepdims=True)
        square_second = jnp.sum(second * second, axis=1, keepdims=True)
        lane = lax.broadcasted_iota(jnp.int32, (HALF, LANES), 1)
        carried = jnp.where((lane >= 64) & (y == 0) & (z == 0), log_sum, 0.0)
        return jnp.where(lane < 32, square_first, jnp.where(lane < 64, square_second, carried))

    each_block = HALF * BLOCK * 4 // 1024

    def end_gather_sends(k):
        wait_kib(ag_send.at[k], len(offsets) * each_block)

    def relay(k, low, high):
        for distance in range(low, high + 1):
            if distance in RELAYED:
                offset_pair = sorted({distance, zn - distance})
                wait_kib(relay_recv.at[k], len(offset_pair) * each_block)
                for dz in offset_pair:
                    block = st.at[k, around(z, dz, zn), x]
                    for dx in across[:-1]:
                        where = dev(s, around(x, dx, xn), y, z)
                        remote(block, block, ag_send.at[k], ag_recv.at[k, distance], where).start()

    def wait_blocks(k, distance):
        count = sum(1 for dz, dx in offsets if ring_distance(dz, zn) == distance)
        if distance in RELAYED:
            count = count * (xn - 1) // xn
        wait_kib(ag_recv.at[k, distance], count * each_block)

    tile_kib = HALF * LANES * 4 // 1024

    def spread_tile(k, tile):
        tl[k, z] = tile
        for dz in range(1, zn):
            copy = remote(tl.at[k, z], tl.at[k, z], y_send.at[0], tl_recv.at[k], dev(s, x, y, around(z, dz, zn)))
            copy.start()

    def pass_tile(k, total):
        ysend[k] = total
        yex[k, y] = total
        for dy in range(1, xn):
            where = dev(s, x, around(y, dy, xn), z)
            remote(ysend.at[k], yex.at[k, y], y_send.at[1], y_recv.at[k], where).start()

    def tile_total(k):
        wait_kib(y_recv.at[k], (xn - 1) * tile_kib)
        return tree(yex[k, j] for j in range(xn))

    def gathered_product(k):
        total = None
        for distance in range(reach + 1):
            wait_blocks(k, distance)
            places = [around(z, dz, zn) for dz in sorted({distance, (zn - distance) % zn})]
            lhs = jnp.concatenate(
                [
                    jnp.concatenate([st[k, z2, g, c] for z2 in places for c in range(width)], axis=1)
                    for g in range(xn)
                ],
                axis=0,
            )
            out = block_product(lhs, k + 1, [pl.multiple_of(z2 * BLOCK, BLOCK) for z2 in places])
            total = out if total is None else [total[0] + out[0], total[1] + out[1]]
        for g in range(xn):
            for o in range(2):
                psend[k, g, :, o * BLOCK : (o + 1) * BLOCK] = total[o][g * HALF : (g + 1) * HALF]

    @pl.when(s == 0)
    def _():
        own_rows.wait()
        for c in range(chunks):
            t_copy(0, c).wait()
            for b in range(t_chunk // BLOCK):
                split_rows(0, c * t_chunk + b * BLOCK)

    pl.semaphore_wait(barrier, peers)

    @pl.when(s == 0)
    def _():
        partner_rows.wait_recv()
        total = None
        for kb in range(zn):
            pieces = [
                jnp.concatenate(
                    [
                        xin[f, pl.ds(g * HALF * stride + kb * width + c, HALF, stride=stride), :]
                        for c in range(width)
                    ],
                    axis=1,
                )
                for f in range(2)
                for g in range(xn)
            ]
            out = block_product(jnp.concatenate(pieces, axis=0), 0, [kb * BLOCK])
            total = out if total is None else [total[0] + out[0], total[1] + out[1]]
        for f in range(2):
            for g in range(xn):
                row = (f * xn + g) * HALF
                for o in range(2):
                    pfirst[f, g, :, o * BLOCK : (o + 1) * BLOCK] = total[o][row : row + HALF]
        reduce_sends(0, pfirst.at[1], 1, False)
        reduce_sends(0, pfirst.at[0], 0, True)
        lend(1, 1, 0)
        for c in range(chunks):
            t_copy(1, c).wait()
        split_site(1)

    @pl.when(s == 1)
    def _():
        own_rows.wait()
        partner_rows.start()
        lend(0, 2, 1)
        for local in range(2):
            for c in range(chunks):
                t_copy(local, c).wait()
            split_site(2 + local)

    own_first = s * fronts + x * HALF
    is_first = outcome_rows(0, HALF, own_first)
    spread_tile(0, reduce_group(0, None, is_first, 0.0))
    relay(0, 1, reach)

    @pl.when(s == 1)
    def _():
        lend(1, 3, 2)
        wait_site(t_recv.at[0])
        split_site(1)

    logs = jnp.zeros((HALF, 1), jnp.float32)
    for k in range(1, STEPS):
        gathered_product(k - 1)
        reduce_sends(k, psend.at[k - 1], s, True)
        wait_kib(tl_recv.at[k - 1], (zn - 1) * tile_kib)
        pass_tile(k - 1, tree(tl[k - 1, j] for j in range(zn)))
        if k < STEPS - 1:

            @pl.when(s == 0)
            def _():
                wait_site(t_recv.at[k])
                split_site(k + 1)

        was_first, is_first = is_first, outcome_rows(k, HALF, own_first)
        scale, more = weigh(tile_total(k - 1), was_first)
        logs = logs + more
        tile = reduce_group(k, scale, is_first, logs if k == STEPS - 1 else 0.0)
        if k < STEPS - 1:
            spread_tile(k, tile)
            relay(k, 1, reach)

    last = STEPS - 1
    pass_tile(last, tile)
    relay(last, 1, 1)
    tlf[z, x] = tile_total(last)
    for dz, dx in offsets:
        where = dev(s, around(x, dx, xn), y, around(z, dz, zn))
        remote(tlf.at[z, x], tlf.at[z, x], y_send.at[2], tl_recv.at[last], where).start()
    relay(last, 2, reach)
    is_first = outcome_rows(last, fronts, s * fronts)
    for distance in range(reach + 1):
        wait_blocks(last, distance)
    wait_kib(tl_recv.at[last], len(offsets) * tile_kib)
    total = jnp.concatenate([tree(tlf[j, g] for j in range(zn)) for g in range(xn)], axis=0)
    scale, logs = weigh(total, is_first)
    for g in range(xn):
        wide_scale = jnp.broadcast_to(scale[g * HALF : (g + 1) * HALF], (HALF, LANES))
        for j in range(zn):
            for c in range(width):
                rows_ref[pl.ds(g * HALF * stride + j * width + c, HALF, stride=stride), :] = (
                    st[last, j, g, c] * wide_scale
                )
    lane = lax.broadcasted_iota(jnp.int32, (fronts, LANES), 1)
    row = lax.broadcasted_iota(jnp.int32, (fronts, LANES), 0)
    log_ref[...] = jnp.sum(jnp.where(lane == row, logs, 0.0), axis=0, keepdims=True)[:, :fronts]

    @pl.when(s == 0)
    def _():
        end_reduce_sends(0, 2 * xn)
        wait_site(t_send.at[0])

    @pl.when(s == 1)
    def _():
        partner_rows.wait_send()
        wait_site(t_send.at[1])
        wait_site(t_send.at[2])

    for k in range(STEPS):
        if k:
            end_reduce_sends(k, xn)
        end_gather_sends(k)
    wait_kib(y_send.at[0], (STEPS - 1) * (zn - 1) * tile_kib)
    wait_kib(y_send.at[1], STEPS * (xn - 1) * tile_kib)
    wait_kib(y_send.at[2], len(offsets) * tile_kib)


def deliver(rows_ref, log_ref, rows_out, log_out, sem):
    copies = (
        pltpu.make_async_copy(rows_ref, rows_out, sem.at[0]),
        pltpu.make_async_copy(log_ref, log_out, sem.at[1]),
    )
    for copy in copies:
        copy.start()
    for copy in copies:
        copy.wait()


def shards(xn, zn, initial_rows, outcomes, tensors):
    fronts, _, rows_k = initial_rows.shape
    bond = xn * rows_k
    dma = pltpu.SemaphoreType.DMA
    vmem = pl.BlockSpec(memory_space=pltpu.VMEM)
    anywhere = pl.BlockSpec(memory_space=pl.ANY)
    f32 = jnp.float32
    lines = fronts * rows_k // LANES
    reach = zn // 2
    rows, logs = pl.pallas_call(
        functools.partial(kernel, xn, zn, float(bond)),
        out_shape=(
            pltpu.VMEM((lines, LANES), f32),
            pltpu.VMEM((1, fronts), f32),
        ),
        in_specs=[anywhere, vmem, anywhere],
        out_specs=(vmem, vmem),
        scratch_shapes=[
            pltpu.VMEM((STEPS, 2, rows_k, BLOCK), f32),
            pltpu.VMEM((STEPS, 2, rows_k, BLOCK), jnp.bfloat16),
            pltpu.VMEM((STEPS, 2, rows_k, BLOCK), jnp.bfloat16),
            pltpu.VMEM((2, lines, LANES), f32),
            pltpu.VMEM((2, xn, HALF, 2 * BLOCK), f32),
            pltpu.VMEM((STEPS - 1, xn, HALF, 2 * BLOCK), f32),
            pltpu.VMEM((STEPS, xn, HALF, 2 * BLOCK), f32),
            pltpu.VMEM((STEPS, zn, xn, 2, HALF, LANES), f32),
            pltpu.VMEM((STEPS - 1, zn, HALF, LANES), f32),
            pltpu.VMEM((zn, xn, HALF, LANES), f32),
            pltpu.VMEM((STEPS, xn, HALF, LANES), f32),
            pltpu.VMEM((STEPS, HALF, LANES), f32),
            dma((2, max(1, rows_k // 512))),
            dma((3,)),
            dma((3,)),
            dma((3,)),
            dma((STEPS,)),
            dma((STEPS,)),
            dma((STEPS,)),
            dma((STEPS, reach + 1)),
            dma((3,)),
            dma((STEPS,)),
            dma((STEPS,)),
            dma((STEPS,)),
        ],
        compiler_params=pltpu.CompilerParams(
            collective_id=0, has_side_effects=True, vmem_limit_bytes=56 * 1024 * 1024
        ),
    )(initial_rows.reshape(lines, LANES), outcomes.T, tensors)
    rows, logs = pl.pallas_call(
        deliver,
        out_shape=(
            jax.ShapeDtypeStruct((lines, LANES), f32),
            jax.ShapeDtypeStruct((1, fronts), f32),
        ),
        in_specs=[vmem, vmem],
        out_specs=(anywhere, anywhere),
        scratch_shapes=[dma((2,))],
    )(pltpu.with_memory_space_constraint(rows, pltpu.VMEM), pltpu.with_memory_space_constraint(logs, pltpu.VMEM))
    return rows.reshape(fronts, 1, rows_k), logs.reshape(fronts)


def solution(mesh):
    xn = mesh.shape["narrow"]
    zn = mesh.shape["wide"] // xn
    return jax.shard_map(
        functools.partial(shards, xn, zn),
        mesh=mesh,
        in_specs=(P("site", "narrow", None), P(), P("site", None, "narrow", None, "wide")),
        out_specs=(P("site", "narrow", None), P("site")),
        check_vma=False,
    )
```
